32 devices in a mesh: dp: 16 (over z, y, core), own: 2 (over x).
Axes of the slice: x: 2, y: 2, z: 4, core: 2. Of those that a mesh axis runs over, the one named last changes fastest.
Arguments:
- tokens: bfloat16 [6144, 2048], P('dp'), may hold values from -6 to 6
- norm_gain: float32 [2048], replicated, may hold values from 0.5 to 1.5
- qkv_codes: bfloat16 [2048, 3, 1024], P('dp', None, 'own'), may hold values from -5 to 5
- qkv_scales: float32 [2048, 3, 8], P('dp', None, 'own'), may hold values from 0.011048543 to 0.044194173
- out_codes: bfloat16 [2048, 1024], P('dp', 'own'), may hold values from -5 to 5
- out_scales: float32 [2048, 8], P('dp', 'own'), may hold values from 0.015625 to 0.0625
- block_mask: int32 [48, 9], P('dp'), may hold values from 0 to 1, as said below
- key_counts: int32 [48], replicated, may hold values from 1 to 128, as said below
- upstream: bfloat16 [6144, 2048], P('dp'), may hold values from -0.076171875 to 0.076171875
Outputs:
- mixed: bfloat16 [6144, 2048], P('dp')
- qkv_grad: float32 [2048, 3, 1024], P('dp', None, 'own')
- out_grad: float32 [2048, 1024], P('dp', 'own')
The draws below stay inside these ranges and needn't reach their ends.
Inputs may be any that keep to these rules, and one draw needn't show every extreme that they name: `block_mask`: the entry of a query block's own block is always 1. `key_counts`: some block is full.
All inputs are finite; a program needn't handle non-finite values.
Results may differ from the reference program's by a relative error of at most 0.035.
Values may be sent and summed in bfloat16 or wider, within the bound.
No kernel may reach another device: no remote copies, remote signals or barrier semaphores. Data moves between devices by JAX's collectives and lax.ppermute only.
A program may use at most 128 MiB of HBM per device.

```python
import math
import jax
import jax.numpy as jnp
from jax import lax

D = 2048
HEAD = 128
HEADS = 8
BLOCK = 128
TOK_DEV = 384
TOKENS = 6144
HW = 1024
BPD = 3
NQB = 48
KBW = 9
N_DP = 16


def draw_block_mask(key, part):
    first, second = jax.random.split(jax.random.fold_in(key, 11))
    level = jax.random.randint(first, (NQB, 1), 0, 4)
    values = jax.random.randint(second, (NQB, KBW), 0, 4)
    picked = (values <= level).astype(jnp.int32)
    rows = jnp.arange(NQB, dtype=jnp.int32)[:, None]
    columns = jnp.arange(KBW, dtype=jnp.int32)[None, :]
    own_block = columns == BPD + rows % BPD
    return jnp.where(own_block, 1, picked).astype(jnp.int32)


def draw_key_counts(key, part):
    first, second = jax.random.split(jax.random.fold_in(key, 23))
    counts = jax.random.randint(first, (NQB,), 1, BLOCK + 1)
    place = jax.random.randint(second, (), 0, NQB)
    return jnp.where(jnp.arange(NQB, dtype=jnp.int32) == place, BLOCK, counts).astype(jnp.int32)


def block_scale(key, dims, pieces, smallest, high):
    def one(dim, shards_of):
        draws = jax.random.uniform(jax.random.fold_in(jax.random.fold_in(key, 6), dim), (shards_of,), jnp.float32, smallest / len(pieces), high / len(pieces))
        return jnp.repeat(jnp.exp(draws), dims[dim] // shards_of).reshape((-1,) + (1,) * (len(dims) - dim - 1))

    gain = one(*pieces[0])
    for cut in pieces[1:]:
        gain = gain * one(*cut)
    return gain


def centred(stream_key, extent, spread, limit, cuts=(), kind=jnp.bfloat16):
    array = jax.random.normal(stream_key, extent, jnp.float32) * spread
    if len(cuts) > 0:
        array = block_scale(stream_key, extent, cuts, -0.22, 0.18) * array
    return jnp.clip(array, min=-limit, max=limit).astype(kind)


def setup_inputs(seed: int = 0) -> dict:
    keys = jax.random.split(jax.random.key(seed), 10)
    tokens = centred(keys[0], (TOKENS, D), 1.0, 6.0, ((0, 16),))
    norm_gain = jnp.clip(1.0 + 0.1 * jax.random.normal(keys[1], (D,), jnp.float32), 0.5, 1.5)
    qkv_codes = centred(keys[2], (D, 3, HW), 1.0, 5.0, ((0, 16), (2, 2)))
    qkv_scales = jnp.clip(jnp.exp(math.log(0.044194173) - 1.3862944 * jax.random.uniform(keys[3], (D, 3, HEADS), jnp.float32) ** block_scale(keys[3], (D, 3, HEADS), ((0, 16), (2, 2)), -0.2, 0.2)), 0.011048543, 0.044194173)
    out_codes = centred(keys[4], (D, HW), 1.0, 5.0, ((0, 16), (1, 2)))
    out_scales = jnp.clip(jnp.exp(math.log(0.0625) - 1.3862944 * jax.random.uniform(keys[5], (D, HEADS), jnp.float32) ** block_scale(keys[5], (D, HEADS), ((0, 16), (1, 2)), -0.2, 0.2)), 0.015625, 0.0625)
    block_mask = draw_block_mask(jax.random.fold_in(keys[9], 71), 0)
    key_counts = draw_key_counts(jax.random.fold_in(keys[9], 71), 0)
    upstream = centred(keys[8], (TOKENS, D), (TOKENS ** -0.5), 0.076171875, ((0, 16),))
    return {"tokens": tokens, "norm_gain": norm_gain, "qkv_codes": qkv_codes, "qkv_scales": qkv_scales, "out_codes": out_codes, "out_scales": out_scales, "block_mask": block_mask, "key_counts": key_counts, "upstream": upstream}


def attend_range(query_rows, key_rows, value_rows, allowed, datt_rows):
    heads = query_rows.shape[1] // HEAD
    inv_root = 1.0 / HEAD ** 0.5
    query_h = query_rows.astype(jnp.float32).reshape(query_rows.shape[0], heads, HEAD)
    key_h = key_rows.astype(jnp.float32).reshape(key_rows.shape[0], heads, HEAD)
    value_h = value_rows.astype(jnp.float32).reshape(value_rows.shape[0], heads, HEAD)
    datt_h = datt_rows.astype(jnp.float32).reshape(datt_rows.shape[0], heads, HEAD)
    scores = jnp.einsum('qhe,khe->hqk', query_h, key_h) * inv_root
    expo = jnp.where(allowed[None], jnp.exp(jnp.where(allowed[None], scores, 0.0)), 0.0)
    probs = expo / lax.optimization_barrier(jnp.sum(expo, axis=-1, keepdims=True))
    probs_b = probs.astype(jnp.bfloat16).astype(jnp.float32)
    attended = jnp.einsum('hqk,khe->qhe', probs_b, value_h).astype(jnp.bfloat16)
    d_prob = jnp.einsum('qhe,khe->hqk', datt_h, value_h)
    delta = lax.optimization_barrier(jnp.sum(probs * d_prob, axis=-1, keepdims=True))
    d_score = (probs * (d_prob - delta) * inv_root).astype(jnp.bfloat16).astype(jnp.float32)
    grad_query = jnp.einsum('hqk,khe->qhe', d_score, key_h).astype(jnp.bfloat16)
    grad_key = jnp.einsum('hqk,qhe->khe', d_score, query_h)
    grad_value = jnp.einsum('hqk,qhe->khe', probs_b, datt_h)
    rows = query_rows.shape[0]
    width = query_rows.shape[1]
    return (attended.reshape(rows, width), grad_query.reshape(rows, width), grad_key.reshape(-1, width), grad_value.reshape(-1, width))

def reference(tokens, norm_gain, qkv_codes, qkv_scales, out_codes, out_scales, block_mask, key_counts, upstream):
    xfloat = tokens.astype(jnp.float32)
    factor = lax.rsqrt(lax.optimization_barrier(jnp.mean(xfloat * xfloat, axis=-1, keepdims=True)) + 1e-05)
    normed = (xfloat * factor * norm_gain[None, :]).astype(jnp.bfloat16)
    w_qkv = (qkv_codes.astype(jnp.float32).reshape(D, 3, HEADS, HEAD) * qkv_scales[..., None]).reshape(D, 3 * HW).astype(jnp.bfloat16)
    w_out = (out_codes.astype(jnp.float32).reshape(D, HEADS, HEAD) * out_scales[..., None]).reshape(D, HW).astype(jnp.bfloat16)
    qkv = jnp.dot(normed, w_qkv, preferred_element_type=jnp.float32).astype(jnp.bfloat16).reshape(TOKENS, 3, HW)
    queries = qkv[:, 0]
    zero_pad = jnp.zeros((TOK_DEV, HW), jnp.bfloat16)
    keys_pad = jnp.concatenate([zero_pad, qkv[:, 1], zero_pad], axis=0)
    values_pad = jnp.concatenate([zero_pad, qkv[:, 2], zero_pad], axis=0)
    counts_pad = jnp.concatenate([jnp.zeros((BPD,), jnp.int32), key_counts, jnp.zeros((BPD,), jnp.int32)])
    d_att = jnp.dot(upstream, w_out, preferred_element_type=jnp.float32).astype(jnp.bfloat16)
    within = jnp.arange(KBW * BLOCK, dtype=jnp.int32) % BLOCK

    def one_range(index):
        index = index.astype(jnp.int32)
        start = (index * TOK_DEV).astype(jnp.int32)
        query_rows = lax.dynamic_slice_in_dim(queries, start, TOK_DEV, 0)
        key_rows = lax.dynamic_slice_in_dim(keys_pad, start, 3 * TOK_DEV, 0)
        value_rows = lax.dynamic_slice_in_dim(values_pad, start, 3 * TOK_DEV, 0)
        datt_rows = lax.dynamic_slice_in_dim(d_att, start, TOK_DEV, 0)
        mask_rows = lax.dynamic_slice_in_dim(block_mask, (index * BPD).astype(jnp.int32), BPD, 0)
        counts_win = lax.dynamic_slice_in_dim(counts_pad, (index * BPD).astype(jnp.int32), KBW, 0)
        live = within < jnp.repeat(counts_win, BLOCK)
        blocks = jnp.repeat(jnp.repeat(mask_rows, BLOCK, axis=0), BLOCK, axis=1) > 0
        allowed = jnp.logical_and(blocks, live[None, :])
        return attend_range(query_rows, key_rows, value_rows, allowed, datt_rows)
    attended, grad_query, grad_key, grad_value = lax.map(one_range, jnp.arange(N_DP, dtype=jnp.int32))
    attended = attended.reshape(TOKENS, HW)
    grad_query = grad_query.reshape(TOKENS, HW)

    def fold_back(parts):
        parts = parts.reshape(N_DP, 3, TOK_DEV, HW)
        zero_one = jnp.zeros((1, TOK_DEV, HW), jnp.float32)
        from_next = jnp.concatenate([parts[1:, 0], zero_one], axis=0)
        from_prev = jnp.concatenate([zero_one, parts[:-1, 2]], axis=0)
        return (parts[:, 1] + from_next + from_prev).astype(jnp.bfloat16).reshape(TOKENS, HW)
    grad_key = fold_back(grad_key)
    grad_value = fold_back(grad_value)
    mixed = jnp.dot(attended, w_out.T, preferred_element_type=jnp.float32).astype(jnp.bfloat16)
    out_grad = jnp.dot(upstream.T, attended, preferred_element_type=jnp.float32)
    d_qkv = jnp.stack([grad_query, grad_key, grad_value], axis=1).reshape(TOKENS, 3 * HW)
    qkv_grad = jnp.dot(normed.T, d_qkv, preferred_element_type=jnp.float32).reshape(D, 3, HW)
    return (mixed, qkv_grad, out_grad)
```

```python
import functools
import math

import jax
import jax.numpy as jnp
from jax import lax
from jax.experimental import pallas as pl
from jax.experimental.pallas import tpu as pltpu
from jax.sharding import PartitionSpec as P

HEAD = 128
INV_ROOT = 1.0 / HEAD**0.5
EXP2_SCALE = INV_ROOT * math.log2(math.e)


NT = (((1,), (1,)), ((), ()))
TN = (((0,), (0,)), ((), ()))
NN = (((1,), (0,)), ((), ()))


def dot(a, b, dims):
    return lax.dot_general(a, b, dims, preferred_element_type=jnp.float32)


def dequant_rows(codes, scales):
    shape = codes.shape
    heads = scales.shape[-1]
    grouped = codes.astype(jnp.float32).reshape(shape[:-1] + (heads, shape[-1] // heads))
    return (grouped * scales[..., None]).reshape(shape).astype(jnp.bfloat16)


def segment(near_ref, left_ref, right_ref, starts, ranges, rows, index):
    if index == 0:
        return left_ref[...]
    if index == ranges + 1:
        return right_ref[...]
    return near_ref[pl.ds(starts[index - 1], rows), :]


def slot_starts(core_ref, ranges, rows):
    if ranges == 1:
        return [0]
    core = core_ref[0]
    return [pl.multiple_of(core * rows, 128), pl.multiple_of((1 - core) * rows, 128)]


def masked_tiles(scores, limit_ref, base, blocks, window, first, fill):
    size = scores.shape[0] // blocks
    row = lax.broadcasted_iota(jnp.int32, (size, size), 0)
    tiles = []
    for b in range(blocks):
        parts = []
        for i in range(blocks):
            tile = scores[b * size : (b + 1) * size, i * size : (i + 1) * size]
            limit = limit_ref[base + i * window + first + b]
            parts.append(jnp.where(row < limit, tile, fill))
        tiles.append(jnp.concatenate(parts, axis=1))
    return jnp.concatenate(tiles, axis=0)


def forward_kernel(
    core_ref, limit_ref, q_ref, k_ref, v_ref, kl_ref, vl_ref, kr_ref, vr_ref, att_ref, lse_ref,
    *, ranges, rows, blocks
):
    window = 3 * blocks
    starts = slot_starts(core_ref, ranges, rows)
    for p in range(ranges):
        query = q_ref[pl.ds(starts[p], rows), :]
        scores = []
        for j in range(3):
            key = segment(k_ref, kl_ref, kr_ref, starts, ranges, rows, p + j)
            scores.append(
                masked_tiles(
                    dot(key, query, NT), limit_ref, p * blocks * window, blocks, window,
                    j * blocks, -jnp.inf,
                )
            )
        peak = functools.reduce(jnp.maximum, [jnp.max(s, axis=0, keepdims=True) for s in scores])
        peak = peak * EXP2_SCALE
        total = jnp.zeros((1, rows), jnp.float32)
        out = jnp.zeros((HEAD, rows), jnp.float32)
        for j in range(3):
            value = segment(v_ref, vl_ref, vr_ref, starts, ranges, rows, p + j)
            expo = jnp.exp2(scores[j] * EXP2_SCALE - peak)
            total = total + jnp.sum(expo, axis=0, keepdims=True)
            out = out + dot(value, expo.astype(jnp.bfloat16), TN)
        out = out * (1.0 / total)
        att_ref[pl.ds(starts[p], rows), :] = out.T.astype(jnp.bfloat16)
        lse_ref[0, p : p + 1, :] = peak + jnp.log2(total)


def backward_kernel(
    core_ref, limit_ref, q_ref, k_ref, v_ref, kl_ref, vl_ref, kr_ref, vr_ref, datt_ref, lse_ref,
    dq_ref, dnear_ref, dleft_ref, dright_ref, *, ranges, rows, blocks
):
    window = 3 * blocks
    starts = slot_starts(core_ref, ranges, rows)
    grads = {}
    for p in range(ranges):
        query = q_ref[pl.ds(starts[p], rows), :]
        datt = datt_ref[pl.ds(starts[p], rows), :]
        lse = lse_ref[0, p : p + 1, :]
        probs, dprobs = [], []
        delta = jnp.zeros((1, rows), jnp.float32)
        for j in range(3):
            key = segment(k_ref, kl_ref, kr_ref, starts, ranges, rows, p + j)
            value = segment(v_ref, vl_ref, vr_ref, starts, ranges, rows, p + j)
            scores = dot(key, query, NT)
            expo = masked_tiles(
                jnp.exp2(scores * EXP2_SCALE - lse), limit_ref, p * blocks * window, blocks,
                window, j * blocks, 0.0,
            )
            dprob = dot(value, datt, NT)
            delta = delta + jnp.sum(expo * dprob, axis=0, keepdims=True)
            probs.append(expo)
            dprobs.append(dprob)
        dquery = jnp.zeros((HEAD, rows), jnp.float32)
        for j in range(3):
            key = segment(k_ref, kl_ref, kr_ref, starts, ranges, rows, p + j)
            dscore = (probs[j] * (dprobs[j] - delta) * INV_ROOT).astype(jnp.bfloat16)
            dquery = dquery + dot(key, dscore, TN)
            pair = (dot(dscore, query, NN), dot(probs[j].astype(jnp.bfloat16), datt, NN))
            if p + j in grads:
                pair = (grads[p + j][0] + pair[0], grads[p + j][1] + pair[1])
            grads[p + j] = pair
        dq_ref[pl.ds(starts[p], rows), :] = dquery.T.astype(jnp.bfloat16)
    for n in range(2):
        dleft_ref[n] = grads[0][n].astype(jnp.bfloat16)
        dright_ref[n] = grads[ranges + 1][n].astype(jnp.bfloat16)
        for p in range(ranges):
            dnear_ref[n, pl.ds(starts[p], rows), :] = grads[p + 1][n]


def attention_specs(ranges, rows, heads):
    smem = pl.BlockSpec(memory_space=pltpu.SMEM)

    def column(length, shift):
        return pl.BlockSpec((length, HEAD), lambda h: (0, h + shift))

    return [
        smem,
        smem,
        column(ranges * rows, 0),
        column(ranges * rows, heads),
        column(ranges * rows, 2 * heads),
        column(rows, 0),
        column(rows, heads),
        column(rows, 0),
        column(rows, heads),
    ]


def attend_forward(core, limits, qkv, left, right, ranges, rows, blocks):
    width = qkv.shape[1] // 3
    heads = width // HEAD
    return pl.pallas_call(
        functools.partial(forward_kernel, ranges=ranges, rows=rows, blocks=blocks),
        grid=(heads,),
        in_specs=attention_specs(ranges, rows, heads),
        out_specs=[
            pl.BlockSpec((ranges * rows, HEAD), lambda h: (0, h)),
            pl.BlockSpec((1, ranges, rows), lambda h: (h, 0, 0)),
        ],
        out_shape=[
            jax.ShapeDtypeStruct((ranges * rows, width), jnp.bfloat16),
            jax.ShapeDtypeStruct((heads, ranges, rows), jnp.float32),
        ],
        name="attend_forward",
    )(core, limits, qkv, qkv, qkv, left, left, right, right)


def attend_backward(core, limits, qkv, left, right, datt, lse, ranges, rows, blocks):
    width = qkv.shape[1] // 3
    heads = width // HEAD
    near = ranges * rows
    return pl.pallas_call(
        functools.partial(backward_kernel, ranges=ranges, rows=rows, blocks=blocks),
        grid=(heads,),
        in_specs=attention_specs(ranges, rows, heads)
        + [
            pl.BlockSpec((near, HEAD), lambda h: (0, h)),
            pl.BlockSpec((1, ranges, rows), lambda h: (h, 0, 0)),
        ],
        out_specs=[
            pl.BlockSpec((near, HEAD), lambda h: (0, h)),
            pl.BlockSpec((2, near, HEAD), lambda h: (0, 0, h)),
            pl.BlockSpec((2, rows, HEAD), lambda h: (0, 0, h)),
            pl.BlockSpec((2, rows, HEAD), lambda h: (0, 0, h)),
        ],
        out_shape=[
            jax.ShapeDtypeStruct((near, width), jnp.bfloat16),
            jax.ShapeDtypeStruct((2, near, width), jnp.float32),
            jax.ShapeDtypeStruct((2, rows, width), jnp.bfloat16),
            jax.ShapeDtypeStruct((2, rows, width), jnp.bfloat16),
        ],
        name="attend_backward",
    )(core, limits, qkv, qkv, qkv, left, left, right, right, datt, lse)


class Ring:
    def __init__(self, devices):
        self.chips = devices // 2
        order = list(range(0, self.chips, 2)) + list(range(self.chips - 1, 0, -2))
        hops = [(order[i], order[(i + 1) % self.chips]) for i in range(self.chips)]
        self.forth = [(2 * a + c, 2 * b + c) for a, b in hops for c in range(2)]
        self.back = [(b, a) for a, b in self.forth]
        table = [[0] * self.chips for _ in range(self.chips)]
        for i, chip in enumerate(order):
            for k in range(self.chips):
                table[chip][k] = order[(i + k) % self.chips]
        chip = lax.axis_index("dp") // 2
        row = lax.dynamic_slice_in_dim(jnp.array(table, jnp.int32), chip, 1, 0)[0]
        self.at = [row[k] for k in range(self.chips)]

    def send(self, block, forward):
        return lax.ppermute(block, "dp", self.forth if forward else self.back)

    def gather(self, block):
        rows = block.shape[0]
        half = rows // 2
        full = jnp.zeros((self.chips * rows,) + block.shape[1:], block.dtype)

        def put(full, part, distance, shift=0):
            start = self.at[distance % self.chips] * rows + shift
            return lax.dynamic_update_slice_in_dim(full, part, start, 0)

        full = put(full, block, 0)
        forth = back = block
        for k in range(1, self.chips // 2):
            forth = self.send(forth, True)
            back = self.send(back, False)
            full = put(put(full, forth, -k), back, k)
        far = self.chips // 2
        forth = self.send(forth[:half], True)
        back = self.send(back[half:], False)
        return put(put(full, forth, far), back, far, half)

    def scatter(self, terms):
        rows = terms.shape[0] // self.chips
        half = rows // 2

        def own(distance, shift=0, size=rows):
            start = self.at[distance % self.chips] * rows + shift
            return lax.dynamic_slice_in_dim(terms, start, size, 0)

        far = self.chips // 2
        forth = self.send(own(far, 0, half), True)
        back = self.send(own(far, half, half), False)
        for k in range(far - 1, 0, -1):
            mine, yours = own(k), own(-k)
            if k == far - 1:
                forth = jnp.concatenate([add(mine[:half], forth), mine[half:]], axis=0)
                back = jnp.concatenate([yours[:half], add(yours[half:], back)], axis=0)
            else:
                forth = add(mine, forth)
                back = add(yours, back)
            forth = self.send(forth, True)
            back = self.send(back, False)
        return own(0).astype(jnp.float32) + forth.astype(jnp.float32) + back.astype(jnp.float32)


def add(a, b):
    return (a.astype(jnp.float32) + b.astype(jnp.float32)).astype(jnp.bfloat16)


def swap_cores(block):
    count = lax.axis_size("dp")
    return lax.ppermute(block, "dp", [(i, i ^ 1) for i in range(count)])


def by_core(core, mine, other, axis):
    return jnp.where(
        core == 0,
        jnp.concatenate([mine, other], axis=axis),
        jnp.concatenate([other, mine], axis=axis),
    )


def per_device(
    tokens, norm_gain, qkv_codes, qkv_scales, out_codes, out_scales, block_mask, key_counts, upstream
):
    rows, depth = tokens.shape
    blocks, window = block_mask.shape
    count = lax.axis_size("dp")
    position = lax.axis_index("dp")
    width = qkv_codes.shape[2]
    split = 2 if (width // HEAD) % 2 == 0 else 1
    core = position % 2 if split == 2 else jnp.int32(0)
    near = width // split
    ring = Ring(count) if split == 2 else None

    w_here = jnp.concatenate(
        [dequant_rows(qkv_codes, qkv_scales), dequant_rows(out_codes, out_scales)[:, None]], axis=1
    )
    if split == 2:
        keep = lax.dynamic_slice_in_dim(w_here, core * near, near, 2)
        give = lax.dynamic_slice_in_dim(w_here, (1 - core) * near, near, 2)
        w_chip = by_core(core, keep, swap_cores(give), 0)
        w_chip = w_chip.reshape(w_chip.shape[0], 4 * near)
        w_qkv = ring.gather(w_chip[:, : 3 * near])
        w_out = ring.gather(w_chip[:, 3 * near :])
    else:
        w_here = w_here.reshape(w_here.shape[0], 4 * near)
        w_all = lax.all_gather(w_here, "dp", axis=0, tiled=True)
        w_qkv, w_out = w_all[:, : 3 * near], w_all[:, 3 * near :]

    xfloat = tokens.astype(jnp.float32)
    factor = lax.rsqrt(jnp.mean(xfloat * xfloat, axis=-1, keepdims=True) + 1e-05)
    normed = (xfloat * factor * norm_gain[None, :]).astype(jnp.bfloat16)
    masks = block_mask[None]
    if split == 2:
        normed = jnp.concatenate([normed, swap_cores(normed)], axis=0)
        upstream = jnp.concatenate([upstream, swap_cores(upstream)], axis=0)
        masks = by_core(core, masks, swap_cores(masks), 0)
    first = position - core
    zeros = jnp.zeros((blocks,), jnp.int32)
    padded = jnp.concatenate([zeros, key_counts, zeros])
    limits = jnp.stack(
        [
            jnp.where(
                masks[p] > 0,
                lax.dynamic_slice_in_dim(padded, (first + p) * blocks, window, 0)[None],
                0,
            )
            for p in range(split)
        ]
    ).reshape(-1)
    core_scalar = core.reshape(1)

    qkv = dot(normed, w_qkv, NN).astype(jnp.bfloat16)
    last = lax.dynamic_slice_in_dim(qkv[:, near:], (1 - core) * rows * (split - 1), rows, 0)
    head = lax.dynamic_slice_in_dim(qkv[:, near:], core * rows, rows, 0)
    up = [(i, i + split) for i in range(count - split)]
    down = [(b, a) for a, b in up]
    left = lax.ppermute(last, "dp", up)
    right = lax.ppermute(head, "dp", down)
    attended, lse = attend_forward(core_scalar, limits, qkv, left, right, split, rows, blocks)

    term_out = dot(upstream, attended, TN)
    mixed = dot(attended[:rows], w_out, NT)
    if split == 2:
        away = swap_cores(dot(attended[rows:], w_out, NT).astype(jnp.bfloat16))
        mixed = mixed + away.astype(jnp.float32)
    mixed = mixed.astype(jnp.bfloat16)
    owners = lax.axis_size("own")
    if owners == 2:
        mixed = add(mixed, lax.ppermute(mixed, "own", [(0, 1), (1, 0)]))
    else:
        mixed = lax.psum(mixed, "own")

    d_att = dot(upstream, w_out, NN).astype(jnp.bfloat16)
    d_query, d_near, d_left, d_right = attend_backward(
        core_scalar, limits, qkv, left, right, d_att, lse, split, rows, blocks
    )
    from_next = lax.ppermute(d_left, "dp", down)
    from_prev = lax.ppermute(d_right, "dp", up)
    if split == 2:
        far = jnp.concatenate(
            [
                jnp.where(core == 0, from_prev, from_next),
                jnp.where(core == 0, from_next, from_prev),
            ],
            axis=1,
        ).astype(jnp.float32)
    else:
        far = from_prev.astype(jnp.float32) + from_next.astype(jnp.float32)
    d_keyval = (d_near + far).astype(jnp.bfloat16)

    if split == 2:

        def finish(block):
            half = block.shape[0] // 2
            keep = lax.dynamic_slice_in_dim(block, core * half, half, 0)
            give = lax.dynamic_slice_in_dim(block, (1 - core) * half, half, 0)
            return by_core(core, keep, swap_cores(give), 1)

        out_grad = finish(ring.scatter(term_out.astype(jnp.bfloat16)))
        grads = [
            finish(ring.scatter(dot(normed, part, TN).astype(jnp.bfloat16)))
            for part in (d_query, d_keyval[0], d_keyval[1])
        ]
        qkv_grad = jnp.stack(grads, axis=1)
    else:
        out_grad = lax.psum_scatter(term_out, "dp", scatter_dimension=0, tiled=True)
        d_qkv = jnp.concatenate([d_query, d_keyval[0], d_keyval[1]], axis=1)
        term_qkv = dot(normed, d_qkv, TN)
        qkv_grad = lax.psum_scatter(term_qkv, "dp", scatter_dimension=0, tiled=True)
        qkv_grad = qkv_grad.reshape(qkv_grad.shape[0], 3, near)
    return (mixed, qkv_grad, out_grad)


def solution(mesh):
    placed = (
        P("dp", None),
        P(),
        P("dp", None, "own"),
        P("dp", None, "own"),
        P("dp", "own"),
        P("dp", "own"),
        P("dp", None),
        P(),
        P("dp", None),
    )
    return jax.shard_map(
        per_device,
        mesh=mesh,
        in_specs=placed,
        out_specs=(P("dp", None), P("dp", None, "own"), P("dp", "own")),
        check_vma=False,
    )
```

```python
import functools
import math

import jax
import jax.numpy as jnp
from jax import lax
from jax.experimental import pallas as pl
from jax.experimental.pallas import tpu as pltpu
from jax.sharding import PartitionSpec as P


HEAD = 128
INV_ROOT = 1.0 / HEAD**0.5
EXP2_SCALE = INV_ROOT * math.log2(math.e)


NT = (((1,), (1,)), ((), ()))
TN = (((0,), (0,)), ((), ()))
NN = (((1,), (0,)), ((), ()))


def dot(a, b, dims):
    return lax.dot_general(a, b, dims, preferred_element_type=jnp.float32)


def dequant_rows(codes, scales):
    shape = codes.shape
    heads = scales.shape[-1]
    grouped = codes.astype(jnp.float32).reshape(shape[:-1] + (heads, shape[-1] // heads))
    return (grouped * scales[..., None]).reshape(shape).astype(jnp.bfloat16)


def place_of(info_ref, ranges, rows):
    core, side = (info_ref[0], info_ref[1]) if ranges == 2 else (0, 0)
    near = [core * rows, (1 - core) * rows][:ranges]
    far = [core * rows, (1 - core) * rows]
    half = rows // 2
    return near, far, [side * half, (1 - side) * half]


def load_segment(near_ref, far_ref, place, ranges, rows, index):
    near, far, halves = place
    if 0 < index <= ranges:
        return near_ref[pl.ds(pl.multiple_of(near[index - 1], 128), rows), :]
    base = far[0 if index == 0 else 1]
    parts = [
        far_ref[pl.ds(pl.multiple_of(base + shift, 64), rows // 2), :] for shift in halves
    ]
    return jnp.concatenate(parts, axis=0)


def masked_tiles(scores, limit_ref, base, blocks, window, first, fill):
    size = scores.shape[0] // blocks
    row = lax.broadcasted_iota(jnp.int32, (size, size), 0)
    tiles = []
    for b in range(blocks):
        parts = []
        for i in range(blocks):
            tile = scores[b * size : (b + 1) * size, i * size : (i + 1) * size]
            limit = limit_ref[base + i * window + first + b]
            parts.append(jnp.where(row < limit, tile, fill))
        tiles.append(jnp.concatenate(parts, axis=1))
    return jnp.concatenate(tiles, axis=0)


def forward_kernel(
    info_ref, limit_ref, q_ref, k_ref, v_ref, kf_ref, vf_ref, att_ref, lse_ref,
    *, ranges, rows, blocks
):
    window = 3 * blocks
    place = place_of(info_ref, ranges, rows)
    for p in range(ranges):
        here = pl.ds(pl.multiple_of(place[0][p], 128), rows)
        query = q_ref[here, :]
        scores = []
        for j in range(3):
            key = load_segment(k_ref, kf_ref, place, ranges, rows, p + j)
            scores.append(
                masked_tiles(
                    dot(key, query, NT), limit_ref, p * blocks * window, blocks, window,
                    j * blocks, -jnp.inf,
                )
            )
        peak = functools.reduce(jnp.maximum, [jnp.max(s, axis=0, keepdims=True) for s in scores])
        peak = peak * EXP2_SCALE
        total = jnp.zeros((1, rows), jnp.float32)
        out = jnp.zeros((HEAD, rows), jnp.float32)
        for j in range(3):
            value = load_segment(v_ref, vf_ref, place, ranges, rows, p + j)
            expo = jnp.exp2(scores[j] * EXP2_SCALE - peak)
            total = total + jnp.sum(expo, axis=0, keepdims=True)
            out = out + dot(value, expo.astype(jnp.bfloat16), TN)
        out = out * (1.0 / total)
        att_ref[here, :] = out.T.astype(jnp.bfloat16)
        lse_ref[0, p : p + 1, :] = peak + jnp.log2(total)


def backward_kernel(
    info_ref, limit_ref, q_ref, k_ref, v_ref, kf_ref, vf_ref, datt_ref, lse_ref,
    near_ref, far_ref, *, ranges, rows, blocks, heads
):
    window = 3 * blocks
    place = place_of(info_ref, ranges, rows)
    head = pl.program_id(0)
    grads = {}

    def lanes(group):
        return pl.ds(pl.multiple_of((group * heads + head) * HEAD, HEAD), HEAD)

    for p in range(ranges):
        here = pl.ds(pl.multiple_of(place[0][p], 128), rows)
        query = q_ref[here, :]
        datt = datt_ref[here, :]
        lse = lse_ref[0, p : p + 1, :]
        probs, dprobs = [], []
        delta = jnp.zeros((1, rows), jnp.float32)
        for j in range(3):
            key = load_segment(k_ref, kf_ref, place, ranges, rows, p + j)
            value = load_segment(v_ref, vf_ref, place, ranges, rows, p + j)
            expo = masked_tiles(
                jnp.exp2(dot(key, query, NT) * EXP2_SCALE - lse), limit_ref,
                p * blocks * window, blocks, window, j * blocks, 0.0,
            )
            dprob = dot(value, datt, NT)
            delta = delta + jnp.sum(expo * dprob, axis=0, keepdims=True)
            probs.append(expo)
            dprobs.append(dprob)
        dquery = jnp.zeros((HEAD, rows), jnp.float32)
        for j in range(3):
            key = load_segment(k_ref, kf_ref, place, ranges, rows, p + j)
            dscore = (probs[j] * (dprobs[j] - delta) * INV_ROOT).astype(jnp.bfloat16)
            dquery = dquery + dot(key, dscore, TN)
            pair = (dot(dscore, query, NN), dot(probs[j].astype(jnp.bfloat16), datt, NN))
            if p + j in grads:
                pair = (grads[p + j][0] + pair[0], grads[p + j][1] + pair[1])
            grads[p + j] = pair
        near_ref[here, lanes(0)] = dquery.T.astype(jnp.bfloat16)
    near, far, halves = place
    half = rows // 2
    for index, pair in grads.items():
        for n in range(2):
            grad = pair[n].astype(jnp.bfloat16)
            if 0 < index <= ranges:
                near_ref[pl.ds(pl.multiple_of(near[index - 1], 128), rows), lanes(n + 1)] = grad
                continue
            base = far[0 if index == 0 else 1]
            for i in range(2):
                start = pl.multiple_of(base + halves[i], 64)
                far_ref[pl.ds(start, half), lanes(n)] = grad[i * half : (i + 1) * half]


def attention_specs(ranges, rows, heads):
    smem = pl.BlockSpec(memory_space=pltpu.SMEM)

    def column(length, shift):
        return pl.BlockSpec((length, HEAD), lambda h: (0, h + shift))

    return [
        smem,
        smem,
        column(ranges * rows, 0),
        column(ranges * rows, heads),
        column(ranges * rows, 2 * heads),
        column(2 * rows, 0),
        column(2 * rows, heads),
    ]


def attend_forward(info, limits, near, far, ranges, rows, blocks):
    width = near.shape[1] // 3
    heads = width // HEAD
    return pl.pallas_call(
        functools.partial(forward_kernel, ranges=ranges, rows=rows, blocks=blocks),
        grid=(heads,),
        in_specs=attention_specs(ranges, rows, heads),
        out_specs=[
            pl.BlockSpec((ranges * rows, HEAD), lambda h: (0, h)),
            pl.BlockSpec((1, ranges, rows), lambda h: (h, 0, 0)),
        ],
        out_shape=[
            jax.ShapeDtypeStruct((ranges * rows, width), jnp.bfloat16),
            jax.ShapeDtypeStruct((heads, ranges, rows), jnp.float32),
        ],
        compiler_params=pltpu.CompilerParams(vmem_limit_bytes=10 << 20),
        name="attend_forward",
    )(info, limits, near, near, near, far, far)


def attend_backward(info, limits, near, far, datt, lse, ranges, rows, blocks):
    heads = near.shape[1] // (3 * HEAD)
    return pl.pallas_call(
        functools.partial(
            backward_kernel, ranges=ranges, rows=rows, blocks=blocks, heads=heads
        ),
        grid=(heads,),
        in_specs=attention_specs(ranges, rows, heads)
        + [
            pl.BlockSpec((ranges * rows, HEAD), lambda h: (0, h)),
            pl.BlockSpec((1, ranges, rows), lambda h: (h, 0, 0)),
        ],
        out_specs=[
            pl.BlockSpec(near.shape, lambda h: (0, 0)),
            pl.BlockSpec(far.shape, lambda h: (0, 0)),
        ],
        out_shape=[
            jax.ShapeDtypeStruct(near.shape, jnp.bfloat16),
            jax.ShapeDtypeStruct(far.shape, jnp.bfloat16),
        ],
        compiler_params=pltpu.CompilerParams(vmem_limit_bytes=24 << 20),
        name="attend_backward",
    )(info, limits, near, near, near, far, far, datt, lse)


def ring_order(chips):
    return list(range(0, chips, 2)) + list(range(chips - 1, 0, -2))


def chip_at(chip, chips, distance):
    spot = jnp.where(chip % 2 == 0, chip // 2, chips - 1 - chip // 2) + distance % chips
    spot = jnp.where(spot >= chips, spot - chips, spot)
    return jnp.where(spot < chips // 2, 2 * spot, 2 * chips - 1 - 2 * spot)


def block_starts(info_ref, chips, distance, block):
    start = chip_at(info_ref[2], chips, distance) * block
    half = block // 2
    core = info_ref[0]
    return (
        pl.multiple_of(start + core * half, 128),
        pl.multiple_of(start + (1 - core) * half, 128),
    )


def ring_hops(devices):
    chips = devices // 2
    order = ring_order(chips)
    hops = [(order[i], order[(i + 1) % chips]) for i in range(chips)]
    forth = [(2 * a + c, 2 * b + c) for a, b in hops for c in range(2)]
    return forth, [(b, a) for a, b in forth]


def both_ways(forth, back):
    ahead, behind = ring_hops(lax.axis_size("dp"))
    forth = lax.ppermute(forth, "dp", ahead)
    back = lax.ppermute(back, "dp", behind)
    return forth, back


def ring_gather(block):
    rows = block.shape[0]
    far = lax.axis_size("dp") // 4
    pieces = [(0, 0, block)]
    forth = back = block
    for k in range(1, far + 1):
        if k == far:
            forth, back = forth[: rows // 2], back[rows // 2 :]
        forth, back = both_ways(forth, back)
        pieces += [(-k, 0, forth), (k, rows // 2 if k == far else 0, back)]
    return pieces


def copy_all(copies):
    for copy in copies:
        copy.start()


def fetch_pieces(info_ref, piece_refs, layout, buffer, sems, first, chips, block, lanes=None):
    copies = []
    half = block // 2
    for n, (ref, (distance, row, size)) in enumerate(zip(piece_refs, layout)):
        starts = block_starts(info_ref, chips, distance, block)
        for part in range(2):
            low, high = max(row, part * half), min(row + size, (part + 1) * half)
            if low >= high:
                continue
            source = ref.at[pl.ds(low - row, high - low), :]
            if lanes is not None and n == 0:
                source = ref.at[pl.ds(low - row, high - low), pl.ds(lanes[0], lanes[1])]
            target = buffer.at[pl.ds(starts[part] + (low - part * half), high - low), :]
            copies.append(pltpu.make_async_copy(source, target, sems.at[first + len(copies)]))
    return copies


def fetch_rows(refs, buffer, sems, first):
    copies, row = [], 0
    for n, ref in enumerate(refs):
        target = buffer.at[pl.ds(row, ref.shape[0]), :]
        copies.append(pltpu.make_async_copy(ref, target, sems.at[first + n]))
        row += ref.shape[0]
    return copies


def piece_layout(pieces):
    return tuple((distance, row, array.shape[0]) for distance, row, array in pieces)


ANY = pl.BlockSpec(memory_space=pl.ANY)
SMEM = pl.BlockSpec(memory_space=pltpu.SMEM)
VMEM = pl.BlockSpec(memory_space=pltpu.VMEM)


def project_kernel(info_ref, *refs, layout, tokens, near, chips, block, near_rows):
    weights, refs = refs[: len(layout)], refs[len(layout) :]
    inputs, (near_ref, far_ref, w_buf, x_buf, sems) = refs[:tokens], refs[tokens:]
    w_copies = fetch_pieces(
        info_ref, weights, layout, w_buf, sems, 0, chips, block, (0, 3 * near)
    )
    x_copies = fetch_rows(inputs, x_buf, sems, len(w_copies))
    copy_all(w_copies)
    copy_all(x_copies)
    for copy in w_copies:
        copy.wait()
    row = 0
    for n, copy in enumerate(x_copies):
        copy.wait()
        size = inputs[n].shape[0]
        rows = x_buf[pl.ds(row, size), :]
        if row < near_rows:
            near_ref[pl.ds(row, size), :] = dot(rows, w_buf[...], NN).astype(jnp.bfloat16)
        else:
            out = dot(rows, w_buf[:, near:], NN)
            far_ref[pl.ds(row - near_rows, size), :] = out.astype(jnp.bfloat16)
        row += size


def project(info, pieces, inputs, near, block, near_rows):
    depth = inputs[0].shape[1]
    total = sum(x.shape[0] for x in inputs)
    layout = piece_layout(pieces)
    kernel = functools.partial(
        project_kernel, layout=layout, tokens=len(inputs), near=near, chips=depth // block,
        block=block, near_rows=near_rows,
    )
    return pl.pallas_call(
        kernel,
        in_specs=[SMEM] + [ANY] * (len(layout) + len(inputs)),
        out_specs=[VMEM, VMEM],
        out_shape=[
            jax.ShapeDtypeStruct((near_rows, 3 * near), jnp.bfloat16),
            jax.ShapeDtypeStruct((total - near_rows, 2 * near), jnp.bfloat16),
        ],
        scratch_shapes=[
            pltpu.VMEM((depth, 3 * near), jnp.bfloat16),
            pltpu.VMEM((total, depth), jnp.bfloat16),
            pltpu.SemaphoreType.DMA((2 * len(layout) + len(inputs),)),
        ],
        compiler_params=pltpu.CompilerParams(vmem_limit_bytes=24 << 20),
        name="project",
    )(info, *[array for _, _, array in pieces], *inputs)


def out_kernel(info_ref, att_ref, *refs, layout, inputs, near, chips, block, lane):
    weights, refs = refs[: len(layout)], refs[len(layout) :]
    sources = refs[:inputs]
    mine_ref, other_ref, datt_ref, term_ref, w_buf, x_buf, sems = refs[inputs:]
    w_copies = fetch_pieces(info_ref, weights, layout, w_buf, sems, 0, chips, block, (lane, near))
    x_copies = fetch_rows(sources, x_buf, sems, len(w_copies))
    copy_all(w_copies)
    copy_all(x_copies)
    for copy in w_copies:
        copy.wait()
    rows = mine_ref.shape[0]
    other_ref[...] = dot(att_ref[rows:, :], w_buf[...], NT).astype(jnp.bfloat16)
    mine_ref[...] = dot(att_ref[:rows, :], w_buf[...], NT).astype(jnp.bfloat16)
    for copy in x_copies:
        copy.wait()
    datt_ref[...] = dot(x_buf[...], w_buf[...], NN).astype(jnp.bfloat16)
    half = block // 2
    for k in range(chips):
        for part, start in enumerate(block_starts(info_ref, chips, k, block)):
            term = dot(x_buf[:, pl.ds(start, half)], att_ref[...], TN)
            term_ref[k * block + part * half : k * block + (part + 1) * half, :] = term.astype(
                jnp.bfloat16
            )


def project_out(info, attended, pieces, inputs, near, block, lane):
    depth = inputs[0].shape[1]
    rows = inputs[0].shape[0]
    total = sum(x.shape[0] for x in inputs)
    layout = piece_layout(pieces)
    kernel = functools.partial(
        out_kernel, layout=layout, inputs=len(inputs), near=near, chips=depth // block,
        block=block, lane=lane,
    )
    return pl.pallas_call(
        kernel,
        in_specs=[SMEM, VMEM] + [ANY] * (len(layout) + len(inputs)),
        out_specs=[VMEM] * 4,
        out_shape=[
            jax.ShapeDtypeStruct((rows, depth), jnp.bfloat16),
            jax.ShapeDtypeStruct((total - rows, depth), jnp.bfloat16),
            jax.ShapeDtypeStruct((total, near), jnp.bfloat16),
            jax.ShapeDtypeStruct((depth, near), jnp.bfloat16),
        ],
        scratch_shapes=[
            pltpu.VMEM((depth, near), jnp.bfloat16),
            pltpu.VMEM((total, depth), jnp.bfloat16),
            pltpu.SemaphoreType.DMA((2 * len(layout) + len(inputs),)),
        ],
        compiler_params=pltpu.CompilerParams(vmem_limit_bytes=24 << 20),
        name="project_out",
    )(info, attended, *[array for _, _, array in pieces], *inputs)


def term_kernel(info_ref, near_ref, far_ref, *refs, tokens, distances, near, chips, block):
    sources, (out_ref, x_buf, sems) = refs[:tokens], refs[tokens:]
    half = block // 2
    copies = []
    for n, distance in enumerate(distances):
        group = []
        for part, start in enumerate(block_starts(info_ref, chips, distance, block)):
            row = 0
            for source in sources:
                size = source.shape[0]
                target = x_buf.at[n, pl.ds(row, size), pl.ds(part * half, half)]
                sem = sems.at[(n * 2 + part) * tokens + len(group) % tokens]
                group.append(
                    pltpu.make_async_copy(source.at[:, pl.ds(start, half)], target, sem)
                )
                row += size
        copies.append(group)
    for group in copies:
        copy_all(group)
    here, there = near_ref[...], far_ref[...]
    rows = here.shape[0]
    for n, group in enumerate(copies):
        for copy in group:
            copy.wait()
        term = dot(x_buf[n, :rows, :], here, TN)
        extra = dot(x_buf[n, rows:, :], there, TN)
        out_ref[n, :, :near] = term[:, :near].astype(jnp.bfloat16)
        out_ref[n, :, near:] = (term[:, near:] + extra).astype(jnp.bfloat16)


def gradient_terms(info, d_near, d_far, inputs, distances, near, block):
    depth = inputs[0].shape[1]
    total = sum(x.shape[0] for x in inputs)
    kernel = functools.partial(
        term_kernel, tokens=len(inputs), distances=distances, near=near, chips=depth // block,
        block=block,
    )
    return pl.pallas_call(
        kernel,
        in_specs=[SMEM, VMEM, VMEM] + [ANY] * len(inputs),
        out_specs=VMEM,
        out_shape=jax.ShapeDtypeStruct((len(distances), block, 3 * near), jnp.bfloat16),
        scratch_shapes=[
            pltpu.VMEM((len(distances), total, block), jnp.bfloat16),
            pltpu.SemaphoreType.DMA((len(distances) * 2 * len(inputs),)),
        ],
        compiler_params=pltpu.CompilerParams(vmem_limit_bytes=16 << 20),
        name="terms",
    )(info, d_near, d_far, *inputs)


def pack_kernel(info_ref, codes_ref, scales_ref, out_ref, out_scales_ref, keep_ref, give_ref):
    rows = codes_ref.shape[1]
    heads = keep_ref.shape[1] // (4 * HEAD)
    core = info_ref[0]
    for which, ref in ((core, keep_ref), (1 - core, give_ref)):
        for h in range(heads):
            head = which * heads + h
            lanes = pl.ds(pl.multiple_of(head * HEAD, HEAD), HEAD)
            for c in range(4):
                if c < 3:
                    code, scale = codes_ref[c, :, lanes], scales_ref[c, pl.ds(head, 1), :]
                else:
                    code, scale = out_ref[:, lanes], out_scales_ref[pl.ds(head, 1), :]
                scale = jnp.broadcast_to(scale, (HEAD, rows)).T
                column = (c * heads + h) * HEAD
                ref[:, column : column + HEAD] = (code.astype(jnp.float32) * scale).astype(
                    jnp.bfloat16
                )


def pack_weights(info, qkv_codes, qkv_scales, out_codes, out_scales):
    rows, width = out_codes.shape
    shape = jax.ShapeDtypeStruct((rows, 2 * width), jnp.bfloat16)
    return pl.pallas_call(
        pack_kernel,
        in_specs=[SMEM] + [VMEM] * 4,
        out_specs=[VMEM, VMEM],
        out_shape=[shape, shape],
        compiler_params=pltpu.CompilerParams(vmem_limit_bytes=8 << 20),
        name="pack",
    )(
        info, jnp.transpose(qkv_codes, (1, 0, 2)), jnp.transpose(qkv_scales, (1, 2, 0)),
        out_codes, out_scales.T,
    )


def add(a, b):
    return (a.astype(jnp.float32) + b.astype(jnp.float32)).astype(jnp.bfloat16)


def swap_cores(block):
    count = lax.axis_size("dp")
    return lax.ppermute(block, "dp", [(i, i ^ 1) for i in range(count)])


def by_core(core, mine, other, axis):
    return jnp.where(
        core == 0,
        jnp.concatenate([mine, other], axis=axis),
        jnp.concatenate([other, mine], axis=axis),
    )


def norm(tokens, gain):
    xfloat = tokens.astype(jnp.float32)
    factor = lax.rsqrt(jnp.mean(xfloat * xfloat, axis=-1, keepdims=True) + 1e-05)
    return (xfloat * factor * gain[None, :]).astype(jnp.bfloat16)


def key_limits(masks, key_counts, first, split):
    blocks, window = masks[0].shape
    zeros = jnp.zeros((blocks,), jnp.int32)
    padded = jnp.concatenate([zeros, key_counts, zeros])
    start = (first * blocks).astype(jnp.uint32)
    counts = lax.dynamic_slice(padded, (start,), (blocks * (split - 1) + window,))
    return jnp.concatenate(
        [
            jnp.where(masks[p] > 0, counts[None, p * blocks : p * blocks + window], 0)
            for p in range(split)
        ]
    ).reshape(-1)


def per_core(
    tokens, norm_gain, qkv_codes, qkv_scales, out_codes, out_scales, block_mask, key_counts, upstream
):
    rows, depth = tokens.shape
    blocks = block_mask.shape[0]
    count = lax.axis_size("dp")
    owners = lax.axis_size("own")
    position = lax.axis_index("dp")
    near = qkv_codes.shape[2] // 2
    block = depth // (count // 2)
    core = position % 2
    side = lax.axis_index("own") if owners == 2 else jnp.int32(0)
    info = jnp.stack([core, side, position // 2])

    hop = [(i, i + 1 if i % 2 else i - 1) for i in range(1, count - 1)]
    if owners == 2:
        start = (side * (rows // 2)).astype(jnp.uint32)
        some = lax.dynamic_slice(tokens, (start, jnp.uint32(0)), (rows // 2, depth))
    else:
        some = tokens
    beyond = [lax.ppermute(norm(some, norm_gain), "dp", hop)]

    keep, give = pack_weights(info, qkv_codes, qkv_scales, out_codes, out_scales)
    w_chip = jnp.concatenate([keep, swap_cores(give)], axis=0)
    w_pieces = ring_gather(w_chip[:, : 3 * near])
    o_pieces = ring_gather(w_chip[:, 3 * near :])

    normed = norm(tokens, norm_gain)
    normed = [normed, swap_cores(normed)]
    upstream = [upstream, swap_cores(upstream)]
    if owners == 2:
        beyond.append(lax.ppermute(beyond[0], "own", [(0, 1), (1, 0)]))
    for n in range(len(beyond)):
        beyond.append(swap_cores(beyond[n]))
    inputs = normed + beyond

    masks = block_mask[None]
    masks = by_core(core, masks, swap_cores(masks), 0)
    limits = key_limits(masks, key_counts, position - core, 2)

    qkv, keyval = project(info, w_pieces, inputs, near, block, 2 * rows)
    attended, lse = attend_forward(info, limits, qkv, keyval, 2, rows, blocks)
    mixed, away, d_att, out_terms = project_out(info, attended, o_pieces, upstream, near, block, 0)
    mixed = add(mixed, swap_cores(away))
    if owners == 2:
        away = lax.ppermute(mixed, "own", [(0, 1), (1, 0)])
        mixed = add(mixed, away)
    else:
        mixed = lax.psum(mixed, "own")
    d_near, d_far = attend_backward(info, limits, qkv, keyval, d_att, lse, 2, rows, blocks)

    chips = count // 2
    far = chips // 2
    half = block // 2
    out_terms = out_terms.reshape(chips, block, near)

    def terms(*distances):
        return gradient_terms(info, d_near, d_far, inputs, distances, near, block)

    def join(mine, yours, forth, back, step):
        if step == 1:
            forth = jnp.concatenate([add(mine[:half], forth), mine[half:]], axis=0)
            back = jnp.concatenate([yours[:half], add(yours[half:], back)], axis=0)
            return forth, back
        return add(mine, forth), add(yours, back)

    out_f, out_b = both_ways(out_terms[far, :half], out_terms[far, half:])
    first = terms(far)[0]
    qkv_f, qkv_b = first[:half], first[half:]
    for step in range(1, far + 1):
        k = far - step
        got_f, got_b = both_ways(qkv_f, qkv_b)
        mine = terms(k, -k) if k else terms(0)
        if step == 1:
            out_f, out_b = lax.optimization_barrier(((out_f, out_b), d_far))[0]
        if k:
            out_f, out_b = join(out_terms[k], out_terms[chips - k], out_f, out_b, step)
            out_f, out_b = both_ways(out_f, out_b)
            qkv_f, qkv_b = join(mine[0], mine[1], got_f, got_b, step)

    def total(term, forth, back):
        return term.astype(jnp.float32) + forth.astype(jnp.float32) + back.astype(jnp.float32)

    def finish(rows_of_chip):
        mine, other = rows_of_chip[:half], swap_cores(rows_of_chip[half:])
        return by_core(core, mine, other, 2)

    out_grad = finish(total(out_terms[0], out_f, out_b)[:, None])[:, 0]
    qkv_grad = finish(total(mine[0], got_f, got_b).reshape(block, 3, near))
    return (mixed, qkv_grad, out_grad)


def whole_heads(
    tokens, norm_gain, qkv_codes, qkv_scales, out_codes, out_scales, block_mask, key_counts, upstream
):
    rows = tokens.shape[0]
    blocks = block_mask.shape[0]
    count = lax.axis_size("dp")
    position = lax.axis_index("dp")
    near = qkv_codes.shape[2]
    info = jnp.zeros((3,), jnp.int32)
    w_here = dequant_rows(qkv_codes, qkv_scales).reshape(qkv_codes.shape[0], 3 * near)
    w_here = jnp.concatenate([w_here, dequant_rows(out_codes, out_scales)], axis=1)
    w_all = lax.all_gather(w_here, "dp", axis=0, tiled=True)
    w_qkv, w_out = w_all[:, : 3 * near], w_all[:, 3 * near :]
    normed = norm(tokens, norm_gain)
    up = [(i, i + 1) for i in range(count - 1)]
    beyond = jnp.concatenate(
        [lax.ppermute(normed, "dp", up), lax.ppermute(normed, "dp", [(b, a) for a, b in up])],
        axis=0,
    )
    limits = key_limits(block_mask[None], key_counts, position, 1)
    qkv = dot(normed, w_qkv, NN).astype(jnp.bfloat16)
    keyval = dot(beyond, w_qkv[:, near:], NN).astype(jnp.bfloat16)
    attended, lse = attend_forward(info, limits, qkv, keyval, 1, rows, blocks)
    mixed = lax.psum(dot(attended, w_out, NT).astype(jnp.bfloat16), "own")
    d_att = dot(upstream, w_out, NN).astype(jnp.bfloat16)
    d_near, d_far = attend_backward(info, limits, qkv, keyval, d_att, lse, 1, rows, blocks)
    term = dot(normed, d_near, TN)
    term = jnp.concatenate([term[:, :near], term[:, near:] + dot(beyond, d_far, TN)], axis=1)
    out_grad = lax.psum_scatter(dot(upstream, attended, TN), "dp", scatter_dimension=0, tiled=True)
    qkv_grad = lax.psum_scatter(term, "dp", scatter_dimension=0, tiled=True)
    return (mixed, qkv_grad.reshape(qkv_grad.shape[0], 3, near), out_grad)


def per_device(*args):
    heads = args[2].shape[2] // HEAD
    ringed = heads % 2 == 0 and lax.axis_size("dp") % 4 == 0
    return per_core(*args) if ringed else whole_heads(*args)


def solution(mesh):
    placed = (
        P("dp", None),
        P(),
        P("dp", None, "own"),
        P("dp", None, "own"),
        P("dp", "own"),
        P("dp", "own"),
        P("dp", None),
        P(),
        P("dp", None),
    )
    return jax.shard_map(
        per_device,
        mesh=mesh,
        in_specs=placed,
        out_specs=(P("dp", None), P("dp", None, "own"), P("dp", "own")),
        check_vma=False,
    )
```

```python
import functools
import math

import jax
import jax.numpy as jnp
from jax import lax
from jax.experimental import pallas as pl
from jax.experimental.pallas import tpu as pltpu
from jax.sharding import PartitionSpec as P


HEAD = 128
INV_ROOT = 1.0 / HEAD**0.5
EXP2_SCALE = INV_ROOT * math.log2(math.e)


NT = (((1,), (1,)), ((), ()))
TN = (((0,), (0,)), ((), ()))
NN = (((1,), (0,)), ((), ()))
PROJECT_VMEM = 20 << 20


def dot(a, b, dims):
    return lax.dot_general(a, b, dims, preferred_element_type=jnp.float32)


def dequant_rows(codes, scales):
    shape = codes.shape
    heads = scales.shape[-1]
    grouped = codes.astype(jnp.float32).reshape(shape[:-1] + (heads, shape[-1] // heads))
    return (grouped * scales[..., None]).reshape(shape).astype(jnp.bfloat16)


def place_of(info_ref, ranges, rows):
    core, side = (info_ref[0], info_ref[1]) if ranges == 2 else (0, 0)
    near = [core * rows, (1 - core) * rows][:ranges]
    far = [core * rows, (1 - core) * rows]
    half = rows // 2
    return near, far, [side * half, (1 - side) * half]


def load_segment(near_ref, far_ref, place, ranges, rows, index):
    near, far, halves = place
    if 0 < index <= ranges:
        return near_ref[pl.ds(pl.multiple_of(near[index - 1], 128), rows), :]
    base = far[0 if index == 0 else 1]
    parts = [
        far_ref[pl.ds(pl.multiple_of(base + shift, 64), rows // 2), :] for shift in halves
    ]
    return jnp.concatenate(parts, axis=0)


def key_limit(info_ref, masks, counts_ref, ranges, blocks, p, i, w):
    allowed = masks[0][i, w]
    if ranges == 2:
        allowed = jnp.where(info_ref[0] == p, allowed, masks[1][i, w])
    index = (info_ref[2] * ranges + p - 1) * blocks + w
    total = counts_ref.shape[0]
    inside = jnp.logical_and(index >= 0, index < total)
    count = counts_ref[jnp.clip(index, 0, total - 1)]
    return jnp.where(jnp.logical_and(inside, allowed > 0), count, 0)


def masked_tiles(scores, limit, blocks, first, fill):
    size = scores.shape[0] // blocks
    row = lax.broadcasted_iota(jnp.int32, (size, size), 0)
    tiles = []
    for b in range(blocks):
        parts = []
        for i in range(blocks):
            tile = scores[b * size : (b + 1) * size, i * size : (i + 1) * size]
            parts.append(jnp.where(row < limit(i, first + b), tile, fill))
        tiles.append(jnp.concatenate(parts, axis=1))
    return jnp.concatenate(tiles, axis=0)


def forward_kernel(
    info_ref, mask_ref, other_mask_ref, counts_ref, q_ref, k_ref, v_ref, kf_ref, vf_ref, att_ref, lse_ref,
    *, ranges, rows, blocks
):
    masks = (mask_ref, other_mask_ref)
    place = place_of(info_ref, ranges, rows)
    for p in range(ranges):
        here = pl.ds(pl.multiple_of(place[0][p], 128), rows)
        limit = functools.partial(key_limit, info_ref, masks, counts_ref, ranges, blocks, p)
        query = q_ref[here, :]
        scores = []
        for j in range(3):
            key = load_segment(k_ref, kf_ref, place, ranges, rows, p + j)
            scores.append(
                masked_tiles(dot(key, query, NT), limit, blocks, j * blocks, -jnp.inf)
            )
        peak = functools.reduce(jnp.maximum, [jnp.max(s, axis=0, keepdims=True) for s in scores])
        peak = peak * EXP2_SCALE
        total = jnp.zeros((1, rows), jnp.float32)
        out = jnp.zeros((HEAD, rows), jnp.float32)
        for j in range(3):
            value = load_segment(v_ref, vf_ref, place, ranges, rows, p + j)
            expo = jnp.exp2(scores[j] * EXP2_SCALE - peak)
            total = total + jnp.sum(expo, axis=0, keepdims=True)
            out = out + dot(value, expo.astype(jnp.bfloat16), TN)
        out = out * (1.0 / total)
        att_ref[here, :] = out.T.astype(jnp.bfloat16)
        lse_ref[0, p : p + 1, :] = peak + jnp.log2(total)


def backward_kernel(
    info_ref, mask_ref, other_mask_ref, counts_ref, q_ref, k_ref, v_ref, kf_ref, vf_ref, datt_ref, lse_ref,
    near_ref, far_ref, *, ranges, rows, blocks, heads
):
    masks = (mask_ref, other_mask_ref)
    place = place_of(info_ref, ranges, rows)
    head = pl.program_id(0)
    grads = {}

    def lanes(group):
        return pl.ds(pl.multiple_of((group * heads + head) * HEAD, HEAD), HEAD)

    for p in range(ranges):
        here = pl.ds(pl.multiple_of(place[0][p], 128), rows)
        limit = functools.partial(key_limit, info_ref, masks, counts_ref, ranges, blocks, p)
        query = q_ref[here, :]
        datt = datt_ref[here, :]
        lse = lse_ref[0, p : p + 1, :]
        probs, dprobs = [], []
        delta = jnp.zeros((1, rows), jnp.float32)
        for j in range(3):
            key = load_segment(k_ref, kf_ref, place, ranges, rows, p + j)
            value = load_segment(v_ref, vf_ref, place, ranges, rows, p + j)
            expo = jnp.exp2(dot(key, query, NT) * EXP2_SCALE - lse)
            expo = masked_tiles(expo, limit, blocks, j * blocks, 0.0)
            dprob = dot(value, datt, NT)
            delta = delta + jnp.sum(expo * dprob, axis=0, keepdims=True)
            probs.append(expo)
            dprobs.append(dprob)
        dquery = jnp.zeros((HEAD, rows), jnp.float32)
        for j in range(3):
            key = load_segment(k_ref, kf_ref, place, ranges, rows, p + j)
            dscore = (probs[j] * (dprobs[j] - delta) * INV_ROOT).astype(jnp.bfloat16)
            dquery = dquery + dot(key, dscore, TN)
            pair = (dot(dscore, query, NN), dot(probs[j].astype(jnp.bfloat16), datt, NN))
            if p + j in grads:
                pair = (grads[p + j][0] + pair[0], grads[p + j][1] + pair[1])
            grads[p + j] = pair
        near_ref[here, lanes(0)] = dquery.T.astype(jnp.bfloat16)
    near, far, halves = place
    half = rows // 2
    for index, pair in grads.items():
        for n in range(2):
            grad = pair[n].astype(jnp.bfloat16)
            if 0 < index <= ranges:
                near_ref[pl.ds(pl.multiple_of(near[index - 1], 128), rows), lanes(n + 1)] = grad
                continue
            base = far[0 if index == 0 else 1]
            for i in range(2):
                start = pl.multiple_of(base + halves[i], 64)
                far_ref[pl.ds(start, half), lanes(n)] = grad[i * half : (i + 1) * half]


def attention_specs(ranges, rows, heads):
    smem = pl.BlockSpec(memory_space=pltpu.SMEM)

    def column(length, shift):
        return pl.BlockSpec((length, HEAD), lambda h: (0, h + shift))

    return [
        smem,
        smem,
        smem,
        smem,
        column(ranges * rows, 0),
        column(ranges * rows, heads),
        column(ranges * rows, 2 * heads),
        column(2 * rows, 0),
        column(2 * rows, heads),
    ]


def attend_forward(info, masks, near, far, ranges, rows):
    blocks = masks[0].shape[0]
    width = near.shape[1] // 3
    heads = width // HEAD
    return pl.pallas_call(
        functools.partial(forward_kernel, ranges=ranges, rows=rows, blocks=blocks),
        grid=(heads,),
        in_specs=attention_specs(ranges, rows, heads),
        out_specs=[
            pl.BlockSpec((ranges * rows, HEAD), lambda h: (0, h)),
            pl.BlockSpec((1, ranges, rows), lambda h: (h, 0, 0)),
        ],
        out_shape=[
            jax.ShapeDtypeStruct((ranges * rows, width), jnp.bfloat16),
            jax.ShapeDtypeStruct((heads, ranges, rows), jnp.float32),
        ],
        compiler_params=pltpu.CompilerParams(vmem_limit_bytes=10 << 20),
        name="attend_forward",
    )(info, *masks, near, near, near, far, far)


def attend_backward(info, masks, near, far, datt, lse, ranges, rows):
    blocks = masks[0].shape[0]
    heads = near.shape[1] // (3 * HEAD)
    return pl.pallas_call(
        functools.partial(
            backward_kernel, ranges=ranges, rows=rows, blocks=blocks, heads=heads
        ),
        grid=(heads,),
        in_specs=attention_specs(ranges, rows, heads)
        + [
            pl.BlockSpec((ranges * rows, HEAD), lambda h: (0, h)),
            pl.BlockSpec((1, ranges, rows), lambda h: (h, 0, 0)),
        ],
        out_specs=[
            pl.BlockSpec(near.shape, lambda h: (0, 0)),
            pl.BlockSpec(far.shape, lambda h: (0, 0)),
        ],
        out_shape=[
            jax.ShapeDtypeStruct(near.shape, jnp.bfloat16),
            jax.ShapeDtypeStruct(far.shape, jnp.bfloat16),
        ],
        compiler_params=pltpu.CompilerParams(vmem_limit_bytes=24 << 20),
        name="attend_backward",
    )(info, *masks, near, near, near, far, far, datt, lse)


def ring_order(chips):
    return list(range(0, chips, 2)) + list(range(chips - 1, 0, -2))


def chip_at(chip, chips, distance):
    spot = jnp.where(chip % 2 == 0, chip // 2, chips - 1 - chip // 2) + distance % chips
    spot = jnp.where(spot >= chips, spot - chips, spot)
    return jnp.where(spot < chips // 2, 2 * spot, 2 * chips - 1 - 2 * spot)


def block_starts(info_ref, chips, distance, block):
    start = chip_at(info_ref[2], chips, distance) * block
    half = block // 2
    core = info_ref[0]
    return (
        pl.multiple_of(start + core * half, 128),
        pl.multiple_of(start + (1 - core) * half, 128),
    )


def ring_hops(devices):
    chips = devices // 2
    order = ring_order(chips)
    hops = [(order[i], order[(i + 1) % chips]) for i in range(chips)]
    forth = [(2 * a + c, 2 * b + c) for a, b in hops for c in range(2)]
    return forth, [(b, a) for a, b in forth]


def both_ways(forth, back):
    ahead, behind = ring_hops(lax.axis_size("dp"))
    forth = lax.ppermute(forth, "dp", ahead)
    back = lax.ppermute(back, "dp", behind)
    return forth, back


def ring_gather(block):
    rows = block.shape[0]
    far = lax.axis_size("dp") // 4
    pieces = [(0, 0, block)]
    forth = back = block
    for k in range(1, far + 1):
        if k == far:
            forth, back = forth[: rows // 2], back[rows // 2 :]
        forth, back = both_ways(forth, back)
        pieces += [(-k, 0, forth), (k, rows // 2 if k == far else 0, back)]
    return pieces


SMEM = pl.BlockSpec(memory_space=pltpu.SMEM)
VMEM = pl.BlockSpec(memory_space=pltpu.VMEM)
HBM = pl.BlockSpec(memory_space=pltpu.HBM)


def join_halves(pieces):
    whole = [(distance, (array,)) for distance, _, array in pieces[:-2]]
    return whole + [(pieces[-1][0], (pieces[-2][2], pieces[-1][2]))]


def read_block(refs, layout, n):
    first = sum(layout[i][1] for i in range(n))
    parts = [refs[first + i][...] for i in range(layout[n][1])]
    return parts[0] if len(parts) == 1 else jnp.concatenate(parts, axis=0)


def read_columns(refs, starts, half):
    parts = [
        jnp.concatenate([ref[:, pl.ds(start, half)] for start in starts], axis=1) for ref in refs
    ]
    return parts[0] if len(parts) == 1 else jnp.concatenate(parts, axis=0)


def project_kernel(info_ref, *refs, layout, owned, tokens, near, chips, block):
    count = sum(n for _, n in layout)
    weights, refs = refs[:count], refs[count:]
    inputs, (near_ref, far_ref) = refs[:tokens], refs[tokens:]
    for group, out_ref, first in ((inputs[:owned], near_ref, 0), (inputs[owned:], far_ref, near)):
        total = None
        for n, (distance, _) in enumerate(layout):
            starts = block_starts(info_ref, chips, distance, block)
            rows = read_columns(group, starts, block // 2)
            term = dot(rows, read_block(weights, layout, n)[:, first:], NN)
            total = term if total is None else total + term
        out_ref[...] = total.astype(jnp.bfloat16)


def project(info, blocks, inputs, owned, near, block):
    depth = inputs[0].shape[1]
    rows = sum(x.shape[0] for x in inputs[:owned])
    total = sum(x.shape[0] for x in inputs)
    arrays = [array for _, parts in blocks for array in parts]
    kernel = functools.partial(
        project_kernel, layout=tuple((d, len(parts)) for d, parts in blocks), owned=owned,
        tokens=len(inputs), near=near, chips=depth // block, block=block,
    )
    return pl.pallas_call(
        kernel,
        in_specs=[SMEM] + [VMEM] * (len(arrays) + len(inputs)),
        out_specs=[VMEM, VMEM],
        out_shape=[
            jax.ShapeDtypeStruct((rows, 3 * near), jnp.bfloat16),
            jax.ShapeDtypeStruct((total - rows, 2 * near), jnp.bfloat16),
        ],
        compiler_params=pltpu.CompilerParams(vmem_limit_bytes=PROJECT_VMEM),
        name="project",
    )(info, *arrays, *inputs)


def out_terms_kernel(info_ref, att_ref, *refs, inputs, chips, block):
    sources, terms = refs[:inputs], refs[inputs:]
    for k, term_ref in enumerate(terms):
        rows = read_columns(sources, block_starts(info_ref, chips, k, block), block // 2)
        term_ref[...] = dot(rows, att_ref[...], TN).astype(jnp.bfloat16)


def out_gradient_terms(info, attended, inputs, block):
    chips = inputs[0].shape[1] // block
    term = jax.ShapeDtypeStruct((block, attended.shape[1]), jnp.bfloat16)
    return pl.pallas_call(
        functools.partial(out_terms_kernel, inputs=len(inputs), chips=chips, block=block),
        in_specs=[SMEM, VMEM] + [VMEM] * len(inputs),
        out_specs=[VMEM] * chips,
        out_shape=[term] * chips,
        compiler_params=pltpu.CompilerParams(vmem_limit_bytes=8 << 20),
        name="out_terms",
    )(info, attended, *inputs)


def out_kernel(info_ref, att_ref, *refs, layout, inputs, chips, block):
    count = sum(n for _, n in layout)
    weights, refs = refs[:count], refs[count:]
    sources, (mine_ref, other_ref, datt_ref) = refs[:inputs], refs[inputs:]
    rows = mine_ref.shape[0]
    half = block // 2
    attended = att_ref[...]
    total = None
    for n, (distance, _) in enumerate(layout):
        starts = block_starts(info_ref, chips, distance, block)
        weight = read_block(weights, layout, n)
        mixed = dot(attended, weight, NT).astype(jnp.bfloat16)
        for part, start in enumerate(starts):
            lanes = slice(part * half, (part + 1) * half)
            mine_ref[:, pl.ds(start, half)] = mixed[:rows, lanes]
            other_ref[:, pl.ds(start, half)] = mixed[rows:, lanes]
        term = dot(read_columns(sources, starts, half), weight, NN)
        total = term if total is None else total + term
    datt_ref[...] = total.astype(jnp.bfloat16)


def project_out(info, attended, blocks, inputs, block):
    depth = inputs[0].shape[1]
    rows = inputs[0].shape[0]
    total = sum(x.shape[0] for x in inputs)
    arrays = [array for _, parts in blocks for array in parts]
    kernel = functools.partial(
        out_kernel, layout=tuple((d, len(parts)) for d, parts in blocks), inputs=len(inputs),
        chips=depth // block, block=block,
    )
    return pl.pallas_call(
        kernel,
        in_specs=[SMEM, VMEM] + [VMEM] * (len(arrays) + len(inputs)),
        out_specs=[VMEM] * 3,
        out_shape=[
            jax.ShapeDtypeStruct((rows, depth), jnp.bfloat16),
            jax.ShapeDtypeStruct((total - rows, depth), jnp.bfloat16),
            jax.ShapeDtypeStruct((total, attended.shape[1]), jnp.bfloat16),
        ],
        compiler_params=pltpu.CompilerParams(vmem_limit_bytes=8 << 20),
        name="project_out",
    )(info, attended, *arrays, *inputs)


def term_kernel(info_ref, near_ref, far_ref, *refs, owned, tokens, distances, near, chips, block):
    sources, terms = refs[:tokens], refs[tokens:]
    half = block // 2
    here, there = near_ref[...], far_ref[...]
    for distance, out_ref in zip(distances, terms):
        starts = block_starts(info_ref, chips, distance, block)
        term = dot(read_columns(sources[:owned], starts, half), here, TN)
        extra = dot(read_columns(sources[owned:], starts, half), there, TN)
        out_ref[:, :near] = term[:, :near].astype(jnp.bfloat16)
        out_ref[:, near:] = (term[:, near:] + extra).astype(jnp.bfloat16)


def gradient_terms(info, d_near, d_far, inputs, owned, distances, near, block):
    depth = inputs[0].shape[1]
    kernel = functools.partial(
        term_kernel, owned=owned, tokens=len(inputs), distances=distances, near=near,
        chips=depth // block, block=block,
    )
    return pl.pallas_call(
        kernel,
        in_specs=[SMEM, VMEM, VMEM] + [VMEM] * len(inputs),
        out_specs=[VMEM] * len(distances),
        out_shape=[jax.ShapeDtypeStruct((block, 3 * near), jnp.bfloat16)] * len(distances),
        compiler_params=pltpu.CompilerParams(vmem_limit_bytes=8 << 20),
        name="terms",
    )(info, d_near, d_far, *inputs)


def fetch_inputs(sources, buffers, sems):
    copies = [
        pltpu.make_async_copy(source, buffer, sems.at[n])
        for n, (source, buffer) in enumerate(zip(sources, buffers))
    ]
    for copy in copies:
        copy.start()
    for copy in copies:
        copy.wait()


def norm_kernel(info_ref, tokens_ref, gain_ref, out_ref, x_buf, gain_buf, sems, *, chunk):
    size = out_ref.shape[0]
    here = pl.ds(pl.multiple_of(info_ref[1] * size, 64), size)
    if size == tokens_ref.shape[0]:
        here = pl.ds(0, size)
    fetch_inputs((tokens_ref.at[here, :], gain_ref), (x_buf, gain_buf), sems)
    gain = gain_buf[...]
    for row in range(0, size, chunk):
        x = x_buf[row : row + chunk, :].astype(jnp.float32)
        factor = lax.rsqrt(jnp.mean(x * x, axis=-1, keepdims=True) + 1e-05)
        out_ref[row : row + chunk, :] = (x * factor * gain).astype(jnp.bfloat16)


def norm_rows(info, tokens, gain, size):
    shape = (size, tokens.shape[1])
    gain = gain[None]
    return pl.pallas_call(
        functools.partial(norm_kernel, chunk=64),
        in_specs=[SMEM, HBM, HBM],
        out_specs=VMEM,
        out_shape=jax.ShapeDtypeStruct(shape, jnp.bfloat16),
        scratch_shapes=[
            pltpu.VMEM(shape, tokens.dtype),
            pltpu.VMEM(gain.shape, gain.dtype),
            pltpu.SemaphoreType.DMA((2,)),
        ],
        compiler_params=pltpu.CompilerParams(vmem_limit_bytes=8 << 20),
        name="norm",
    )(info, tokens, gain)


def pack_kernel(info_ref, *refs):
    sources, (keep_ref, keep_out_ref, give_ref), buffers, sems = (
        refs[:4], refs[4:7], refs[7:11], refs[11]
    )
    fetch_inputs(sources, buffers, sems)
    codes_ref, scales_ref, out_ref, out_scales_ref = buffers
    rows = codes_ref.shape[1]
    heads = keep_out_ref.shape[1] // HEAD
    core = info_ref[0]
    for kept in (False, True):
        for h in range(heads):
            head = (core if kept else 1 - core) * heads + h
            lanes = pl.ds(pl.multiple_of(head * HEAD, HEAD), HEAD)
            for c in range(4):
                if c < 3:
                    code, scale = codes_ref[c, :, lanes], scales_ref[c, pl.ds(head, 1), :]
                else:
                    code, scale = out_ref[:, lanes], out_scales_ref[pl.ds(head, 1), :]
                scale = jnp.broadcast_to(scale, (HEAD, rows)).T
                weight = (code.astype(jnp.float32) * scale).astype(jnp.bfloat16)
                column = (c * heads + h) * HEAD
                if not kept:
                    give_ref[:, column : column + HEAD] = weight
                elif c < 3:
                    keep_ref[:, column : column + HEAD] = weight
                else:
                    keep_out_ref[:, h * HEAD : (h + 1) * HEAD] = weight


def pack_weights(info, qkv_codes, qkv_scales, out_codes, out_scales):
    rows, width = out_codes.shape
    sources = (
        jnp.transpose(qkv_codes, (1, 0, 2)), jnp.transpose(qkv_scales, (1, 2, 0)),
        out_codes, out_scales.T,
    )
    shapes = ((rows, 3 * width // 2), (rows, width // 2), (rows, 2 * width))
    return pl.pallas_call(
        pack_kernel,
        in_specs=[SMEM] + [HBM] * 4,
        out_specs=[VMEM] * 3,
        out_shape=[jax.ShapeDtypeStruct(shape, jnp.bfloat16) for shape in shapes],
        scratch_shapes=[pltpu.VMEM(x.shape, x.dtype) for x in sources]
        + [pltpu.SemaphoreType.DMA((4,))],
        compiler_params=pltpu.CompilerParams(vmem_limit_bytes=8 << 20),
        name="pack",
    )(info, *sources)


def add(a, b):
    return (a.astype(jnp.float32) + b.astype(jnp.float32)).astype(jnp.bfloat16)


OUTER_HOPS = ((1, 2), (2, 1), (13, 14), (14, 13))
INNER_HOPS = ((5, 6), (6, 5), (9, 10), (10, 9))
FIRST_LEGS = ((3, 7), (4, 6), (7, 11), (8, 4), (11, 9), (12, 8))
SECOND_LEGS = ((7, 4), (6, 3), (11, 8), (4, 7), (9, 12), (8, 11))


def merge_kernel(info_ref, early_ref, inner_ref, relayed_ref, out_ref):
    device = 2 * info_ref[2] + info_ref[0]
    outer = functools.reduce(jnp.logical_or, [device == to for _, to in OUTER_HOPS])

    @pl.when(outer)
    def _():
        out_ref[...] = early_ref[...]

    @pl.when(jnp.logical_not(outer))
    def _():
        out_ref[...] = inner_ref[...] + relayed_ref[...]


def hop_tokens(info, some, count):
    if count != 16:
        hop = [(i, i + 1 if i % 2 else i - 1) for i in range(1, count - 1)]
        return lax.ppermute(some, "dp", hop)
    early = lax.ppermute(some, "dp", FIRST_LEGS + OUTER_HOPS)
    inner = lax.ppermute(some, "dp", INNER_HOPS)
    relayed = lax.ppermute(early, "dp", SECOND_LEGS)
    return pl.pallas_call(
        merge_kernel,
        in_specs=[SMEM] + [VMEM] * 3,
        out_specs=VMEM,
        out_shape=jax.ShapeDtypeStruct(some.shape, some.dtype),
        compiler_params=pltpu.CompilerParams(vmem_limit_bytes=4 << 20),
        name="merge",
    )(info, early, inner, relayed)


def add(a, b):
    return (a.astype(jnp.float32) + b.astype(jnp.float32)).astype(jnp.bfloat16)


def swap_cores(block):
    count = lax.axis_size("dp")
    return lax.ppermute(block, "dp", [(i, i ^ 1) for i in range(count)])


def by_core(core, mine, other, axis):
    return jnp.where(
        core == 0,
        jnp.concatenate([mine, other], axis=axis),
        jnp.concatenate([other, mine], axis=axis),
    )


def norm(tokens, gain):
    xfloat = tokens.astype(jnp.float32)
    factor = lax.rsqrt(jnp.mean(xfloat * xfloat, axis=-1, keepdims=True) + 1e-05)
    return (xfloat * factor * gain[None, :]).astype(jnp.bfloat16)


def per_core(
    tokens, norm_gain, qkv_codes, qkv_scales, out_codes, out_scales, block_mask, key_counts, upstream
):
    rows, depth = tokens.shape
    count = lax.axis_size("dp")
    owners = lax.axis_size("own")
    position = lax.axis_index("dp")
    near = qkv_codes.shape[2] // 2
    block = depth // (count // 2)
    core = position % 2
    side = lax.axis_index("own") if owners == 2 else jnp.int32(0)
    info = jnp.stack([core, side, position // 2])

    some = norm_rows(info, tokens, norm_gain, rows // 2 if owners == 2 else rows)
    beyond = [hop_tokens(info, some, count)]
    keep, keep_out, give = pack_weights(info, qkv_codes, qkv_scales, out_codes, out_scales)
    got = swap_cores(give)
    w_blocks = join_halves(ring_gather(jnp.concatenate([keep, got[:, : 3 * near]], axis=0)))
    o_blocks = join_halves(ring_gather(jnp.concatenate([keep_out, got[:, 3 * near :]], axis=0)))
    normed = norm_rows(info, tokens, norm_gain, rows)
    normed = [normed, swap_cores(normed)]
    upstream = [upstream, swap_cores(upstream)]
    if owners == 2:
        beyond.append(lax.ppermute(beyond[0], "own", [(0, 1), (1, 0)]))
    for n in range(len(beyond)):
        beyond.append(swap_cores(beyond[n]))
    inputs = normed + beyond

    masks = (block_mask, swap_cores(block_mask), key_counts)

    qkv, keyval = project(info, w_blocks, inputs, len(normed), near, block)
    attended, lse = attend_forward(info, masks, qkv, keyval, 2, rows)
    out_terms = out_gradient_terms(info, attended, upstream, block)
    mixed, away, d_att = project_out(info, attended, o_blocks, upstream, block)
    mixed = add(mixed, swap_cores(away))
    if owners == 2:
        away = lax.ppermute(mixed, "own", [(0, 1), (1, 0)])
        mixed = add(mixed, away)
    else:
        mixed = lax.psum(mixed, "own")
    d_near, d_far = attend_backward(info, masks, qkv, keyval, d_att, lse, 2, rows)

    chips = count // 2
    far = chips // 2
    half = block // 2

    def terms(*distances):
        return gradient_terms(
            info, d_near, d_far, inputs, len(normed), distances, near, block
        )

    def join(mine, yours, forth, back, step):
        if step == 1:
            forth = jnp.concatenate([add(mine[:half], forth), mine[half:]], axis=0)
            back = jnp.concatenate([yours[:half], add(yours[half:], back)], axis=0)
            return forth, back
        return add(mine, forth), add(yours, back)

    out_f, out_b = both_ways(out_terms[far][:half], out_terms[far][half:])
    for step in range(1, far):
        k = far - step
        out_f, out_b = join(out_terms[k], out_terms[chips - k], out_f, out_b, step)
        out_f, out_b = both_ways(out_f, out_b)
    mine = terms(far)[0]
    qkv_f, qkv_b = both_ways(mine[:half], mine[half:])
    for step in range(1, far):
        k = far - step
        mine = terms(k, -k)
        qkv_f, qkv_b = join(mine[0], mine[1], qkv_f, qkv_b, step)
        qkv_f, qkv_b = both_ways(qkv_f, qkv_b)
    mine = terms(0)[0]

    def total(term, forth, back):
        return term.astype(jnp.float32) + forth.astype(jnp.float32) + back.astype(jnp.float32)

    def finish(rows_of_chip):
        mine, give = rows_of_chip[:, :half], rows_of_chip[:, half:].astype(jnp.bfloat16)
        other = swap_cores(give).astype(jnp.float32)
        return by_core(core, mine, other, 2)

    out_grad = finish(total(out_terms[0], out_f, out_b)[None])[0]
    mine = total(mine, qkv_f, qkv_b)
    mine = jnp.stack([mine[:, c * near : (c + 1) * near] for c in range(3)])
    qkv_grad = jnp.transpose(finish(mine), (1, 0, 2))
    return (mixed, qkv_grad, out_grad)


def whole_heads(
    tokens, norm_gain, qkv_codes, qkv_scales, out_codes, out_scales, block_mask, key_counts, upstream
):
    rows = tokens.shape[0]
    count = lax.axis_size("dp")
    position = lax.axis_index("dp")
    near = qkv_codes.shape[2]
    info = jnp.stack([jnp.int32(0), jnp.int32(0), position])
    w_here = dequant_rows(qkv_codes, qkv_scales).reshape(qkv_codes.shape[0], 3 * near)
    w_here = jnp.concatenate([w_here, dequant_rows(out_codes, out_scales)], axis=1)
    w_all = lax.all_gather(w_here, "dp", axis=0, tiled=True)
    w_qkv, w_out = w_all[:, : 3 * near], w_all[:, 3 * near :]
    normed = norm(tokens, norm_gain)
    up = [(i, i + 1) for i in range(count - 1)]
    beyond = jnp.concatenate(
        [lax.ppermute(normed, "dp", up), lax.ppermute(normed, "dp", [(b, a) for a, b in up])],
        axis=0,
    )
    masks = (block_mask, block_mask, key_counts)
    qkv = dot(normed, w_qkv, NN).astype(jnp.bfloat16)
    keyval = dot(beyond, w_qkv[:, near:], NN).astype(jnp.bfloat16)
    attended, lse = attend_forward(info, masks, qkv, keyval, 1, rows)
    mixed = lax.psum(dot(attended, w_out, NT).astype(jnp.bfloat16), "own")
    d_att = dot(upstream, w_out, NN).astype(jnp.bfloat16)
    d_near, d_far = attend_backward(info, masks, qkv, keyval, d_att, lse, 1, rows)
    term = dot(normed, d_near, TN)
    term = jnp.concatenate([term[:, :near], term[:, near:] + dot(beyond, d_far, TN)], axis=1)
    out_grad = lax.psum_scatter(dot(upstream, attended, TN), "dp", scatter_dimension=0, tiled=True)
    qkv_grad = lax.psum_scatter(term, "dp", scatter_dimension=0, tiled=True)
    return (mixed, qkv_grad.reshape(qkv_grad.shape[0], 3, near), out_grad)


def per_device(*args):
    heads = args[2].shape[2] // HEAD
    ringed = heads % 2 == 0 and lax.axis_size("dp") % 4 == 0
    return per_core(*args) if ringed else whole_heads(*args)


def solution(mesh):
    placed = (
        P("dp", None),
        P(),
        P("dp", None, "own"),
        P("dp", None, "own"),
        P("dp", "own"),
        P("dp", "own"),
        P("dp", None),
        P(),
        P("dp", None),
    )
    return jax.shard_map(
        per_device,
        mesh=mesh,
        in_specs=placed,
        out_specs=(P("dp", None), P("dp", None, "own"), P("dp", "own")),
        check_vma=False,
    )
```
